32 devices in a mesh: groups: 2 (over x), cand: 16 (over z, y, core).
Axes of the slice: x: 2, y: 2, z: 4, core: 2. Of those that a mesh axis runs over, the one named last changes fastest.
Arguments:
- cand_rows: bfloat16 [24576, 1024], P(('groups', 'cand')), parts along dimension 0, may hold values from -6 to 6
- user_rows: bfloat16 [192, 1024], P(('groups', 'cand')), parts along dimension 0, may hold values from -6 to 6
- counts: int32 [192], P(('groups', 'cand')), parts along dimension 0, may hold values from 16 to 512, as said below
- starts: int32 [192], P(('groups', 'cand')), parts along dimension 0, may hold values from 0 to 47, as said below
- norm_gain: float32 [1024], replicated, may hold values from 0.1 to 1.9
- w_cand: bfloat16 [1024, 1024], replicated, may hold values from -0.1875 to 0.1875
- w_user: bfloat16 [1024, 1024], replicated, may hold values from -0.1875 to 0.1875
- w_query: bfloat16 [1024, 1024], replicated, may hold values from -0.25 to 0.25
- w_key: bfloat16 [1024, 1024], replicated, may hold values from -0.25 to 0.25
- w_value: bfloat16 [1024, 1024], replicated, may hold values from -0.1875 to 0.1875
- w_out: bfloat16 [1024, 1024], replicated, may hold values from -0.1875 to 0.1875
- w_score: float32 [1024], replicated, may hold values from -0.1875 to 0.1875
Outputs:
- score: float32 [24576], P(('groups', 'cand')), parts along dimension 0
The draws below stay inside these ranges and needn't reach their ends.
There are 2 independent parts, one for each index of `groups`. The reference program is written for one: setup_inputs(seed, part) draws one part's arguments, and reference() takes and returns one part's arrays. A program takes and returns all parts, laid end to end along the dimension named above; an argument that names none is the same for every part. Nothing has to cross between parts.
Inputs may be any that keep to these rules, and one draw needn't show every extreme that they name: Within a shard the requests' first tiles increase. Each request's tiles run from its first tile to the next request's first tile; for a shard's last request, to the shard's end and then through the next shard's tiles before that shard's first request. On shard 0 the first request starts at tile 0, elsewhere at most 8 tiles in, which some shard reaches; the last shard's last request ends with the shard and starts at its last tile. `counts`: each count is at most the rows of its request's tiles; some request has exactly 512.
All inputs are finite; a program needn't handle non-finite values.
Results may differ from the reference program's by a relative error of at most 0.0045.
Values may be sent and summed in bfloat16 or wider, within the bound.
No kernel may reach another device: no remote copies, remote signals or barrier semaphores. Data moves between devices by JAX's collectives and lax.ppermute only.
A program may use at most 128 MiB of HBM per device.

```python
import jax
import jax.numpy as jnp
from jax import lax

D = 1024
HEADS = 8
CAND_DEV = 768
REQ_DEV = 6
TILE = 16
MAXC = 512
MINC = 16
SPILL = 128
TOTAL = 12288
REQS = 96
N_CAND = 16


def layout(key):
    shards = N_CAND
    tiles = CAND_DEV // TILE
    long_tiles = MAXC // TILE
    spill_tiles = SPILL // TILE
    key = jax.random.fold_in(key, 7)
    keys = jax.random.split(key, 4)
    shard_ids = jnp.arange(shards, dtype=jnp.int32)
    spill_in = jax.random.randint(keys[0], (shards,), 0, spill_tiles + 1)
    forced = jax.random.randint(keys[1], (), 1, shards)
    spill_in = jnp.where(shard_ids == forced, spill_tiles, spill_in)
    spill_in = jnp.where(shard_ids == 0, 0, spill_in).astype(jnp.int32)
    spill_out = jnp.concatenate([spill_in[1:], jnp.zeros((1,), jnp.int32)])
    heavy_shard = jax.random.randint(keys[2], (), 0, shards)

    def one_shard(shard_key, s_in, s_out, shard):
        sub = jax.random.split(shard_key, 4)
        avail = tiles - long_tiles - s_in
        tile_ids = jnp.arange(tiles, dtype=jnp.int32)
        raw = jax.random.randint(sub[0], (tiles,), 0, 1 << 20)
        ranking = jnp.where((tile_ids >= 1) & (tile_ids < avail), raw * tiles + tile_ids, -1 - tile_ids)
        is_last = shard == shards - 1
        ranking = jnp.where(is_last & (tile_ids == avail - 1), 1 << 30, ranking)
        picked = lax.top_k(ranking, REQ_DEV - 1)[1].astype(jnp.int32)
        cuts = jnp.sort(picked)
        relative = jnp.concatenate([jnp.zeros((1,), jnp.int32), cuts])
        long_any = jax.random.randint(sub[1], (), 0, REQ_DEV)
        long_early = jax.random.randint(sub[3], (), 0, REQ_DEV - 1)
        long_index = jnp.where(is_last, long_early, long_any)
        slots = jnp.arange(REQ_DEV, dtype=jnp.int32)
        firsts = relative + s_in + long_tiles * (slots > long_index).astype(jnp.int32)
        ends = jnp.concatenate([firsts[1:], (tiles + s_out)[None]])
        span = (ends - firsts) * TILE
        amounts = jax.random.randint(sub[2], (REQ_DEV,), MINC, jnp.minimum(span, MAXC) + 1)
        amounts = jnp.where((shard == heavy_shard) & (slots == long_index), MAXC, amounts)
        return (firsts.astype(jnp.int32), amounts.astype(jnp.int32))
    firsts, amounts = jax.vmap(one_shard)(jax.random.split(keys[3], shards), spill_in, spill_out, shard_ids)
    return (firsts.reshape(-1), amounts.reshape(-1))


def draw_counts(key, part):
    return layout(key)[1]


def draw_starts(key, part):
    return layout(key)[0]


def draw_cand_rows(key, part):
    key = jax.random.fold_in(key, 11)
    keys = jax.random.split(key, 3)
    rows = jax.random.normal(keys[2], (TOTAL, D), jnp.float32)
    return jnp.clip(rows, -6.0, 6.0).astype(jnp.bfloat16)


def paired_weights(key):
    key = jax.random.fold_in(key, 23)
    keys = jax.random.split(key, 2)
    base = jax.random.normal(keys[0], (D, D), jnp.float32)
    extra = jax.random.normal(keys[1], (D, D), jnp.float32)
    limit = 8.0 * D ** (-0.5)
    scale = D ** (-0.5)
    query_weight = base * scale
    key_weight = extra * scale
    return (jnp.clip(query_weight, -limit, limit), jnp.clip(key_weight, -limit, limit))


def draw_w_query(key, part):
    return paired_weights(key)[0].astype(jnp.bfloat16)


def draw_w_key(key, part):
    return paired_weights(key)[1].astype(jnp.bfloat16)


def steps_of(own_key, extent, pieces, smallest, largest):
    level, own = 1.0, jax.random.fold_in(own_key, 6)
    for dim, parts in pieces:
        steps = jnp.exp(jax.random.uniform(jax.random.fold_in(own, dim), (parts,), jnp.float32, smallest / len(pieces), largest / len(pieces)))
        level = level * jnp.repeat(steps, extent[dim] // parts).reshape([-1 if axis == dim else 1 for axis in range(len(extent))])
    return level


def bell_draw(stream_key, extent, deviation, most, cuts=(), kind=jnp.bfloat16):
    gain = steps_of(stream_key, extent, cuts, -0.22, 0.18) if cuts else 1.0
    values = jax.random.normal(stream_key, extent, jnp.float32) * deviation * gain
    return jnp.minimum(jnp.maximum(values, -most), most).astype(kind)


def setup_inputs(seed: int = 0, part: int = 0) -> dict:
    splits = jax.random.split(jax.random.key(seed), 13)
    part_keys = jax.random.split(jax.random.fold_in(splits[12], part), 13)
    cand_rows = draw_cand_rows(jax.random.fold_in(jax.random.fold_in(splits[12], part), 71), part)
    user_rows = bell_draw(part_keys[1], (REQS, D), 1.0, 6.0, ((0, 16),))
    counts = draw_counts(jax.random.fold_in(jax.random.fold_in(splits[12], part), 71), part)
    starts = draw_starts(jax.random.fold_in(jax.random.fold_in(splits[12], part), 71), part)
    norm_gain = jnp.clip(1.0 + 0.18 * jax.random.normal(splits[4], (D,), jnp.float32), 0.1, 1.9)
    w_cand = bell_draw(splits[5], (D, D), D ** -0.5, 0.1875)
    w_user = bell_draw(splits[6], (D, D), D ** -0.5, 0.1875)
    w_query = draw_w_query(jax.random.fold_in(splits[12], 71), part)
    w_key = draw_w_key(jax.random.fold_in(splits[12], 71), part)
    w_value = bell_draw(splits[9], (D, D), D ** -0.5, 0.1875)
    w_out = bell_draw(splits[10], (D, D), D ** -0.5, 0.1875)
    w_score = bell_draw(splits[11], (D,), D ** -0.5, 0.1875, (), jnp.float32)
    return dict(cand_rows=cand_rows, user_rows=user_rows, counts=counts, starts=starts, norm_gain=norm_gain, w_cand=w_cand, w_user=w_user, w_query=w_query, w_key=w_key, w_value=w_value, w_out=w_out, w_score=w_score)


def attend(queries, q_labels, key_rows, value_rows, k_labels, head_count):
    head_size = queries.shape[1] // head_count
    allowed = (q_labels[:, None] == k_labels[None, :]) & (q_labels[:, None] >= 0)

    def one_head(head_index):
        col_start = head_index * head_size
        q_part = lax.dynamic_slice_in_dim(queries, col_start, head_size, 1)
        k_part = lax.dynamic_slice_in_dim(key_rows, col_start, head_size, 1)
        v_part = lax.dynamic_slice_in_dim(value_rows, col_start, head_size, 1)
        scores = lax.dot_general(q_part, k_part, (((1,), (1,)), ((), ())), preferred_element_type=jnp.float32)
        scores = jnp.where(allowed, scores * head_size ** (-0.5), -1e+30)
        row_max = lax.optimization_barrier(jnp.max(scores, axis=1, keepdims=True))
        weights = jnp.exp(scores - row_max)
        row_sum = lax.optimization_barrier(jnp.sum(weights, axis=1, keepdims=True))
        softmax_weights = (weights / row_sum).astype(jnp.bfloat16)
        return jnp.dot(softmax_weights, v_part, preferred_element_type=jnp.float32).astype(jnp.bfloat16)
    mixture = lax.map(one_head, jnp.arange(head_count))
    return jnp.transpose(mixture, (1, 0, 2)).reshape(queries.shape[0], head_count * head_size)

def reference(cand_rows, user_rows, counts, starts, norm_gain, w_cand, w_user, w_query, w_key, w_value, w_out, w_score):
    shards = N_CAND
    user_term = jnp.dot(user_rows, w_user, preferred_element_type=jnp.float32).astype(jnp.bfloat16)
    first_grid = (starts * TILE).reshape(shards, REQ_DEV)
    count_grid = counts.reshape(shards, REQ_DEV)
    term_grid = user_term.reshape(shards, REQ_DEV, D)
    prev_first = jnp.concatenate([jnp.zeros((1,), jnp.int32), first_grid[:-1, -1]])
    prev_count = jnp.concatenate([jnp.zeros((1,), jnp.int32), count_grid[:-1, -1]])
    prev_term = jnp.concatenate([jnp.zeros((1, D), jnp.bfloat16), term_grid[:-1, -1]])

    def prepare(inputs):
        block, firsts, amounts, terms, p_first, p_count, p_term = inputs
        position = jnp.arange(CAND_DEV, dtype=jnp.int32)
        holder = lax.optimization_barrier(jnp.sum((position[:, None] >= firsts[None, :]).astype(jnp.int32), axis=1)) - 1
        chosen = holder[:, None] == jnp.arange(REQ_DEV, dtype=jnp.int32)[None, :]
        row_first = lax.optimization_barrier(jnp.sum(jnp.where(chosen, firsts[None, :], 0), axis=1))
        row_count = lax.optimization_barrier(jnp.sum(jnp.where(chosen, amounts[None, :], 0), axis=1))
        usable = jnp.where(holder >= 0, position - row_first < row_count, position + CAND_DEV - p_first < p_count)
        labels = jnp.where(usable, holder + 1, -1)
        user_sel = jnp.dot(chosen.astype(jnp.bfloat16), terms, preferred_element_type=jnp.float32)
        user_sel = user_sel + jnp.where(holder[:, None] < 0, p_term[None, :].astype(jnp.float32), 0.0)
        features = block.astype(jnp.float32)
        mean_square = lax.optimization_barrier(jnp.mean(features * features, axis=1, keepdims=True))
        normed = (features * lax.rsqrt(mean_square + 1e-06) * norm_gain[None, :]).astype(jnp.bfloat16)
        pre_act = jnp.dot(normed, w_cand, preferred_element_type=jnp.float32) + user_sel
        hidden = (features + jax.nn.silu(pre_act)).astype(jnp.bfloat16)
        queries = jnp.dot(hidden, w_query, preferred_element_type=jnp.float32).astype(jnp.bfloat16)
        key_rows = jnp.dot(hidden, w_key, preferred_element_type=jnp.float32).astype(jnp.bfloat16)
        value_rows = jnp.dot(hidden, w_value, preferred_element_type=jnp.float32).astype(jnp.bfloat16)
        return (hidden, queries, jnp.concatenate([key_rows, value_rows], axis=1), labels, usable)
    blocks = cand_rows.reshape(shards, CAND_DEV, D)
    hidden, queries, key_value, labels, usable = lax.map(prepare, (blocks, first_grid, count_grid, term_grid, prev_first, prev_count, prev_term))
    lower_rim = jnp.concatenate([jnp.zeros((1, MAXC, 2 * D), jnp.bfloat16), key_value[:-1, CAND_DEV - MAXC:]], axis=0)
    upper_rim = jnp.concatenate([key_value[1:, :MAXC], jnp.zeros((1, MAXC, 2 * D), jnp.bfloat16)], axis=0)

    def finish(inputs):
        hid, qry, kval, low, upp, labs, keep, firsts, amounts, p_first, p_count = inputs
        offsets = jnp.arange(MAXC, dtype=jnp.int32)
        lower_pos = CAND_DEV - MAXC + offsets - p_first
        lower_labels = jnp.where((lower_pos >= 0) & (lower_pos < p_count), 0, -1)
        upper_labels = jnp.where(CAND_DEV + offsets - firsts[REQ_DEV - 1] < amounts[REQ_DEV - 1], REQ_DEV, -1)
        key_labels = jnp.concatenate([lower_labels, labs, upper_labels])
        widened = jnp.concatenate([low, kval, upp], axis=0)
        mixture = attend(qry, labs, widened[:, :D], widened[:, D:], key_labels, HEADS)
        mixture = jnp.where(keep[:, None], mixture, jnp.zeros_like(mixture))
        combined = hid.astype(jnp.float32) + jnp.dot(mixture, w_out, preferred_element_type=jnp.float32)
        score = lax.optimization_barrier(jnp.sum(combined * w_score[None, :], axis=1))
        return jnp.where(keep, score, 0.0)
    scores = lax.map(finish, (hidden, queries, key_value, lower_rim, upper_rim, labels, usable, first_grid, count_grid, prev_first, prev_count))
    return scores.reshape(TOTAL)
```

```python
import functools
import math

import jax
import jax.numpy as jnp
from jax import lax
from jax.experimental import pallas as pl
from jax.experimental.pallas import tpu as pltpu
from jax.sharding import PartitionSpec as P

HEADS = 8
TILE = 16
SPILL = 128
MAXC = 512
BLK = 128
EPS = 1e-06
NEG = -1e30
F32 = jnp.float32
BF16 = jnp.bfloat16
LIMIT1 = 12
LIMIT2 = 14
LIMIT3 = 8
NT = (((1,), (1,)), ((), ()))


def passed_along(block, axis, distance):
    devices = range(lax.axis_size(axis))
    route = [(i - distance, i) for i in devices if i - distance in devices]
    return lax.ppermute(block, axis, route)


def three_pieces(x):
    hi = x.astype(BF16)
    rest = x - hi.astype(F32)
    mid = rest.astype(BF16)
    return hi, mid, (rest - mid.astype(F32)).astype(BF16)


def normed_rows(rows, gain):
    features = rows.astype(F32)
    mean_square = jnp.mean(features * features, axis=1, keepdims=True)
    return (features * lax.rsqrt(mean_square + EPS) * gain).astype(BF16)


def gated(rows, half):
    return ((rows.astype(F32) + half) + half * jnp.tanh(half)).astype(BF16)


def copies_in(pairs, sems):
    copies = [pltpu.make_async_copy(a, b, sems.at[i]) for i, (a, b) in enumerate(pairs)]
    for copy in copies:
        copy.start()
    return copies


def put(ref, rows, cols, value):
    head = ref.shape[2]
    value = value.astype(BF16)
    for h in range(cols.start // head, cols.stop // head):
        ref[h, rows, :] = value[:, h * head - cols.start : (h + 1) * head - cols.start]


def scale_of(head):
    return math.log2(math.e) * head**-0.5


def edge_kernel(cand, edge, sem):
    copy = pltpu.make_async_copy(cand.at[pl.ds(0, edge.shape[0])], edge, sem)
    copy.start()
    copy.wait()


def first_kernel(
    h_starts, w_query, users, gain, w_score, cand, w_user, w_cand, w_out, w_value,
    hidden, folded, terms, queries,
    starts, v_normed, sems,
):
    (copy,) = copies_in([(h_starts, starts)], sems)
    reqs, width = users.shape
    local = cand.shape[0]
    head = width // HEADS

    def norm(parts):
        for part in parts:
            rows = slice(part * BLK, (part + 1) * BLK)
            v_normed[rows, :] = normed_rows(cand[rows, :], 0.5 * gain[...])

    parts = local // BLK
    pieces = three_pieces(w_score[...])
    score_rows = jnp.concatenate([*pieces, jnp.zeros((5, width), BF16)], axis=0)
    out_fold = lax.dot_general(score_rows, w_out[...], NT, preferred_element_type=F32)
    user_term = jnp.dot(users[...], w_user[...], preferred_element_type=F32)
    norm(range(0, parts // 3))
    out_fold = jnp.sum(out_fold, axis=0, keepdims=True)
    norm(range(parts // 3, 2 * parts // 3))
    own_head = lax.broadcasted_iota(jnp.int32, (HEADS, width), 1) // head
    own_head = own_head == lax.broadcasted_iota(jnp.int32, (HEADS, width), 0)
    blocks = jnp.concatenate(three_pieces(jnp.where(own_head, out_fold, 0.0)), axis=0)
    value_fold = lax.dot_general(blocks, w_value[...], NT, preferred_element_type=F32)
    terms[...] = 0.5 * user_term.astype(BF16).astype(F32)
    norm(range(2 * parts // 3, parts))
    value_fold = value_fold[:HEADS] + value_fold[HEADS : 2 * HEADS] + value_fold[2 * HEADS :]
    folded[...] = jnp.concatenate([*three_pieces(value_fold), score_rows], axis=0)
    copy.wait()

    step = width // 4
    columns = [slice(col, col + step) for col in range(0, width, step)]
    holders = []
    for tile in range(local // TILE):
        holder = jnp.int32(0)
        for j in range(1, reqs):
            holder = holder + (starts[j] <= tile).astype(jnp.int32)
        holders.append(holder)

    def product(cols):
        return jnp.dot(v_normed[...], w_cand[:, cols], preferred_element_type=F32)

    def finish(cols, pre):
        for tile, holder in enumerate(holders):
            rows = slice(tile * TILE, (tile + 1) * TILE)
            hidden[rows, cols] = gated(
                cand[rows, cols], pre[rows] + terms[pl.ds(holder, 1), cols]
            )

    pres = [product(columns[0])]
    for n, cols in enumerate(columns):
        if n + 1 < len(columns):
            pres.append(product(columns[n + 1]))
        finish(cols, pres[n])
    for cols in columns:
        query = jnp.dot(hidden[...], w_query[:, cols], preferred_element_type=F32)
        put(queries, slice(0, local), cols, query * scale_of(head))


def attend_step(
    now_blocks, then_blocks, now_near, begin, shift, q_start, spans, q_ref, k_ref, s_ref, top_ref
):
    head = k_ref.shape[2]
    start = pl.multiple_of(begin, TILE)
    q_start = pl.multiple_of(q_start, TILE)
    head_row = lax.broadcasted_iota(jnp.int32, (HEADS, BLK), 0)
    key_row = lax.broadcasted_iota(jnp.int32, (BLK, 1), 0)
    nothing = jnp.zeros((BLK, head), BF16)
    total = jnp.zeros((HEADS, BLK), F32)
    if then_blocks == 1:
        keys_in = lax.broadcasted_iota(jnp.int32, (BLK, 2 * BLK), 0)
        queries_in = lax.broadcasted_iota(jnp.int32, (1, 2 * BLK), 1) % BLK + shift
        key_owner = jnp.zeros((BLK, 2 * BLK), jnp.int32)
        query_owner = jnp.full((1, 2 * BLK), -1, jnp.int32)
        for j, (low, high) in enumerate(spans):
            key_owner = jnp.where((keys_in >= low) & (keys_in < high), j + 1, key_owner)
            query_owner = jnp.where((queries_in >= low) & (queries_in < high), j + 1, query_owner)
        together = key_owner == query_owner
    for pair in range(HEADS // 2):
        if then_blocks:
            q_one, q_two = (q_ref[2 * pair + side, pl.ds(q_start, BLK), :] for side in range(2))
            q_diag = jnp.concatenate(
                [
                    jnp.concatenate([q_one, nothing], axis=1),
                    jnp.concatenate([nothing, q_two], axis=1),
                ],
                axis=0,
            )
            rows = pl.ds(start, then_blocks * BLK)
            k_pair = jnp.concatenate([k_ref[2 * pair, rows, :], k_ref[2 * pair + 1, rows, :]], axis=1)
            scores = lax.dot_general(k_pair, q_diag, NT, preferred_element_type=F32)
        if now_blocks:
            keys = now_blocks * BLK
            weights = jnp.exp2(s_ref[pair, :keys, :] - top_ref[pair : pair + 1, :]).astype(BF16)
        if then_blocks:
            top = jnp.full((1, 2 * BLK), NEG, F32)
            for b in range(then_blocks):
                block = scores[b * BLK : (b + 1) * BLK]
                if then_blocks == 1:
                    block = jnp.where(together, block, NEG)
                elif b >= then_blocks // 2:
                    block = jnp.where(key_row >= spans[-1] - b * BLK, NEG, block)
                top = jnp.maximum(top, jnp.max(block, axis=0, keepdims=True))
                s_ref[pair, b * BLK : (b + 1) * BLK, :] = block
            top_ref[pair : pair + 1, :] = top
        if now_blocks:
            sums = jnp.dot(now_near[:, :keys], weights, preferred_element_type=F32)
            mixed = sums[:HEADS] + sums[HEADS : 2 * HEADS] + sums[2 * HEADS : 3 * HEADS]
            mixed = mixed / sums[3 * HEADS :]
            total = jnp.where(head_row == 2 * pair, mixed[:, :BLK], total)
            total = jnp.where(head_row == 2 * pair + 1, mixed[:, BLK:], total)
    return jnp.sum(total, axis=0, keepdims=True)


def size_of(j, counts):
    reqs = counts.shape[0]
    count = counts[jnp.clip(j, 0, reqs - 1)]
    size = 1 + (count > BLK).astype(jnp.int32) + (count > 2 * BLK).astype(jnp.int32)
    return jnp.where((j < 0) | (j >= reqs), 0, size)


SIZES = (0, 1, 2, MAXC // BLK)


def spans_from(begin, starts, counts):
    lows = [starts[j] * TILE - begin for j in range(starts.shape[0])]
    return [(low, low + counts[j]) for j, low in enumerate(lows)]


def second_kernel(
    h_starts, h_counts, own, spill, gain, terms, folded, w_cand, w_query, w_key,
    k_ref, near_ref, direct, edge,
    starts, counts, v_hidden, q_ref, z_ref, s_ref, top_ref, sems,
):
    local, width = own.shape
    copies = copies_in(
        [(own, v_hidden.at[pl.ds(0, local)]), (h_starts, starts), (h_counts, counts)], sems
    )
    reqs = starts.shape[0]
    head = width // HEADS
    total = local + SPILL
    step = 2 * head
    columns = [slice(col, col + step) for col in range(0, width, step)]

    normed = normed_rows(spill[...], 0.5 * gain[...])
    pre = jnp.dot(normed, w_cand[...], preferred_element_type=F32)
    z_ref[...] = jnp.zeros(z_ref.shape, F32)
    near_ref[...] = jnp.ones(near_ref.shape, BF16)
    spilled = gated(spill[...], pre + terms[reqs - 1 :, :])
    v_hidden[local:, :] = spilled
    for copy in copies:
        copy.wait()

    def all_keys(cols):
        key = jnp.dot(v_hidden[...], w_key[:, cols], preferred_element_type=F32)
        put(k_ref, slice(0, total), cols, key)

    row_terms = lax.dot_general(v_hidden[...], folded[...], NT, preferred_element_type=F32)
    all_keys(columns[0])
    blocks = total // BLK
    directs = []
    for b in range(blocks):
        flat = jnp.transpose(row_terms[b * BLK : (b + 1) * BLK])
        values = flat[:HEADS] + flat[HEADS : 2 * HEADS] + flat[2 * HEADS : 3 * HEADS]
        directs.append(jnp.sum(flat[3 * HEADS :], axis=0, keepdims=True))
        for n, piece in enumerate(three_pieces(values)):
            z_ref[b, n * HEADS : (n + 1) * HEADS, :] = piece.astype(F32)
    all_keys(columns[1])
    place = lax.broadcasted_iota(jnp.int32, (8, BLK), 0) * BLK
    place = place + lax.broadcasted_iota(jnp.int32, (8, BLK), 1)
    live = place < 0
    for low, high in spans_from(0, starts, counts):
        live = live | ((place >= low) & (place < high))
    directs.append(jnp.zeros((8 - blocks, BLK), F32))
    direct[...] = jnp.where(live, jnp.concatenate(directs, axis=0), 0.0)
    query = jnp.dot(v_hidden[local:, :], w_query[...], preferred_element_type=F32)
    put(q_ref, slice(0, SPILL), slice(0, width), query * scale_of(head))
    lanes = lax.broadcasted_iota(jnp.int32, (3 * HEADS, BLK), 1)
    for j in range(reqs):
        first = starts[j] * TILE
        turn = first % BLK
        ahead = [
            pltpu.roll(
                z_ref[jnp.minimum(first // BLK + b, z_ref.shape[0] - 1)], (BLK - turn) % BLK, 1
            )
            for b in range(MAXC // BLK + 1)
        ]
        for b in range(MAXC // BLK):
            near_ref[j, : 3 * HEADS, b * BLK : (b + 1) * BLK] = jnp.where(
                lanes < BLK - turn, ahead[b], ahead[b + 1]
            ).astype(BF16)
    all_keys(columns[2])
    all_keys(columns[3])
    last = reqs - 1
    begin = starts[last] * TILE
    spans = spans_from(begin, starts, counts)
    lane = lax.broadcasted_iota(jnp.int32, (1, BLK), 1)
    edge[...] = jnp.zeros((1, BLK), F32)

    @pl.when(begin + counts[last] > local)
    def _():
        def whole(blocks):
            step_of = functools.partial(
                attend_step, now_near=near_ref.at[last], begin=begin, shift=local - begin,
                q_start=0, spans=spans if blocks == 1 else [counts[last]],
                q_ref=q_ref, k_ref=k_ref, s_ref=s_ref, top_ref=top_ref,
            )
            step_of(0, blocks)
            return step_of(blocks, 0)

        result = lax.switch(
            size_of(jnp.int32(last), counts) - 1,
            [functools.partial(whole, blocks) for blocks in SIZES[1:]],
        )
        rows = local // BLK
        result = result + direct[rows : rows + 1, :]
        edge[...] = jnp.where(local + lane < begin + counts[last], result, 0.0)


def third_kernel(
    h_starts, h_counts, q_ref, k_ref, near_ref, direct,
    scores,
    starts, counts, out, s_ref, top_ref, sems,
):
    copies = copies_in([(h_starts, starts), (h_counts, counts)], sems)
    reqs = starts.shape[0]
    local = scores.shape[0] * BLK
    out[...] = direct[...]
    lane = lax.broadcasted_iota(jnp.int32, (1, BLK), 1)
    for copy in copies:
        copy.wait()

    def one_step(state):
        now, now_shift, then, then_shift = state
        last = jnp.minimum(then, reqs - 1)
        held = jnp.maximum(now, 0)
        begin = starts[last] * TILE
        spans = spans_from(begin, starts, counts)
        step_of = functools.partial(
            attend_step, now_near=near_ref.at[held], begin=begin, shift=then_shift,
            q_start=begin + then_shift, q_ref=q_ref, k_ref=k_ref, s_ref=s_ref, top_ref=top_ref,
        )

        def step_with(a, b):
            return step_of(a, b, spans=spans if b == 1 else [counts[last]])

        result = lax.switch(
            size_of(now, counts),
            [
                functools.partial(
                    lax.switch, size_of(then, counts),
                    [functools.partial(step_with, a, b) for b in SIZES],
                )
                for a in SIZES
            ],
        )
        now_begin = starts[held] * TILE + now_shift
        mine = lane < 0
        for j, (low, high) in enumerate(spans_from(now_begin, starts, counts)):
            inside = (lane >= low) & (lane < high)
            mine = mine | (inside & (j >= now) & ((j < then) | (j == now)))
        result = jnp.where(mine & (lane < local - now_begin), result, 0.0)
        turn = now_begin % BLK
        row = now_begin // BLK
        result = pltpu.roll(result, turn, 1)
        out[pl.ds(row, 1), :] += jnp.where(lane >= turn, result, 0.0)
        out[pl.ds(row + 1, 1), :] += jnp.where(lane < turn, result, 0.0)
        more = then_shift + BLK < jnp.minimum(counts[last], local - begin)
        after = then + 1
        for j, (_, high) in enumerate(spans):
            joins = (j > then) & (high <= BLK) & (counts[last] <= BLK)
            after = after + joins.astype(jnp.int32)
        return (
            then, then_shift, jnp.where(more, then, after), jnp.where(more, then_shift + BLK, 0)
        )

    zero = jnp.int32(0)
    lax.while_loop(
        lambda state: state[0] < reqs, one_step, (jnp.int32(-1), zero, zero, zero)
    )
    scores[...] = out[: scores.shape[0], :]


def per_device(
    cand_rows, user_rows, counts, starts, norm_gain, w_cand, w_user, w_query, w_key, w_value,
    w_out, w_score,
):
    local, width = cand_rows.shape
    total = local + SPILL
    gain = norm_gain[None, :]
    vmem = pl.BlockSpec(memory_space=pltpu.VMEM)
    hbm = pl.BlockSpec(memory_space=pltpu.HBM)
    edge_rows = pl.pallas_call(
        edge_kernel,
        out_shape=jax.ShapeDtypeStruct((SPILL, width), BF16),
        in_specs=[hbm],
        out_specs=vmem,
        scratch_shapes=[pltpu.SemaphoreType.DMA(())],
        compiler_params=pltpu.CompilerParams(vmem_limit_bytes=1 << 20),
        cost_estimate=pl.CostEstimate(flops=1 << 34, bytes_accessed=1 << 24, transcendentals=0),
        name="edge",
    )(pltpu.with_memory_space_constraint(cand_rows, pltpu.HBM))
    spill = passed_along(edge_rows, "cand", -1)
    anywhere = pl.BlockSpec(memory_space=pl.ANY)
    ints = pltpu.SMEM(counts.shape, jnp.int32)
    own_blocks = local // BLK
    head = width // HEADS
    reqs = counts.shape[0]
    softmax_scratch = [
        pltpu.VMEM((HEADS // 2, MAXC, 2 * BLK), F32), pltpu.VMEM((8, 2 * BLK), F32),
    ]
    hidden, folded, terms, queries = pl.pallas_call(
        first_kernel,
        out_shape=(
            jax.ShapeDtypeStruct((local, width), BF16),
            jax.ShapeDtypeStruct((4 * HEADS, width), BF16),
            jax.ShapeDtypeStruct(user_rows.shape, F32),
            jax.ShapeDtypeStruct((HEADS, total, head), BF16),
        ),
        in_specs=[anywhere] + [vmem] * 9,
        out_specs=(vmem,) * 4,
        scratch_shapes=[ints, pltpu.VMEM((local, width), BF16), pltpu.SemaphoreType.DMA((2,))],
        compiler_params=pltpu.CompilerParams(vmem_limit_bytes=LIMIT1 << 20),
        cost_estimate=pl.CostEstimate(
            flops=4 * local * width * width, bytes_accessed=12 << 20, transcendentals=local * width
        ),
        name="fold_and_hidden",
    )(
        starts, w_query,
        user_rows, gain, w_score[None, :], cand_rows, w_user, w_cand, w_out, w_value,
    )
    keys, near, direct, edge = pl.pallas_call(
        second_kernel,
        out_shape=(
            jax.ShapeDtypeStruct((HEADS, total + MAXC, head), BF16),
            jax.ShapeDtypeStruct((reqs, 4 * HEADS, MAXC), BF16),
            jax.ShapeDtypeStruct((8, BLK), F32),
            jax.ShapeDtypeStruct((1, BLK), F32),
        ),
        in_specs=[anywhere] * 2 + [vmem] * 8,
        out_specs=(vmem,) * 4,
        scratch_shapes=[
            ints, ints, pltpu.VMEM((total, width), BF16), pltpu.VMEM((HEADS, SPILL, head), BF16),
            pltpu.VMEM((total // BLK + 1, 3 * HEADS, BLK), F32), *softmax_scratch,
            pltpu.SemaphoreType.DMA((3,)),
        ],
        compiler_params=pltpu.CompilerParams(vmem_limit_bytes=LIMIT2 << 20),
        cost_estimate=pl.CostEstimate(
            flops=4 * total * width * width, bytes_accessed=8 << 20, transcendentals=0
        ),
        name="keys_and_edge",
    )(starts, counts, hidden, spill, gain, terms, folded, w_cand, w_query, w_key)
    received = passed_along(edge, "cand", 1)
    scores = pl.pallas_call(
        third_kernel,
        out_shape=jax.ShapeDtypeStruct((own_blocks, BLK), F32),
        in_specs=[anywhere] * 2 + [vmem] * 4,
        out_specs=vmem,
        scratch_shapes=[
            ints, ints, pltpu.VMEM((8, BLK), F32), *softmax_scratch,
            pltpu.SemaphoreType.DMA((2,)),
        ],
        compiler_params=pltpu.CompilerParams(vmem_limit_bytes=LIMIT3 << 20),
        cost_estimate=pl.CostEstimate(
            flops=4 * total * width * width, bytes_accessed=8 << 20, transcendentals=total * MAXC * 8
        ),
        name="rank",
    )(starts, counts, queries, keys, near, direct)
    first = jnp.where(jnp.arange(own_blocks)[:, None] == 0, received, 0.0)
    return (scores + first).reshape(local)


def solution(mesh):
    in_specs = (
        P(("groups", "cand"), None),
        P(("groups", "cand"), None),
        P(("groups", "cand")),
        P(("groups", "cand")),
        P(), P(), P(), P(), P(), P(), P(), P(),
    )
    return jax.shard_map(
        per_device, mesh=mesh, in_specs=in_specs, out_specs=P(("groups", "cand")), check_vma=False
    )
```
